1024 devices in a mesh: path: 32 (over y, z_hi), fsdp: 32 (over z_lo, x, core).
Axes of the slice: x: 8, y: 8, z: 8 (z_hi: 4, z_lo: 2; z = z_hi * 2 + z_lo), core: 2. Of those that a mesh axis runs over, the one named last changes fastest.
Arguments:
- tokens: bfloat16 [32, 8192, 4096], P('path', 'fsdp'), may hold values from -6 to 6
- cotangent: bfloat16 [32, 8192, 256], P('path', 'fsdp'), may hold values from -6 to 6
- module_table: int32 [32, 1], replicated, may hold values from 0 to 7
- module_weights: bfloat16 [8, 4096, 256], P(None, 'fsdp'), may hold values from -6 to 6
- momentum: float32 [8, 4096, 256], P(None, 'fsdp'), may hold values from -6 to 6
Outputs:
- new_weights: bfloat16 [8, 4096, 256], P(None, 'fsdp')
- new_momentum: float32 [8, 4096, 256], P(None, 'fsdp')
The draws below stay inside these ranges and needn't reach their ends.
Inputs may be any that keep to these rules, and one draw needn't show every extreme that they name: `module_table`: every module is taken by at least one path.
All inputs are finite; a program needn't handle non-finite values.
Results may differ from the reference program's by a relative error of at most 0.0034.
Values may be sent and summed in bfloat16 or wider, within the bound.
A program may use at most 32 MiB of HBM per device.

```python
import math
import jax
import jax.numpy as jnp
from jax import lax

D = 4096
R = 256
MODS = 8
PATHS = 32
PATH_TOKENS = 8192


def block_scale(stream_key, extent, shards, low, largest):
    level, own = 1.0, jax.random.fold_in(stream_key, 6)
    for dim, shards_of in shards:
        draws = jnp.exp(jax.random.uniform(jax.random.fold_in(own, dim), (shards_of,), jnp.float32, low / len(shards), largest / len(shards)))
        level = level * jnp.repeat(draws, extent[dim] // shards_of).reshape([-1 if axis == dim else 1 for axis in range(len(extent))])
    return level


def different_ones(key, rows, count, top, lift):
    ranking = jax.random.permutation(jax.random.fold_in(key, 1), count)
    boost = ranking
    for power in range(3):
        boost = boost * boost // count
    boost = boost * lift // count
    chance = jax.random.randint(jax.random.fold_in(key, 2), (rows, count), 0, 4096) + boost
    fixed_rows = jax.random.permutation(jax.random.fold_in(key, 3), rows)[jnp.arange(count) % rows]
    chance = jnp.where(jnp.arange(rows)[:, None] == fixed_rows[None, :], 1 << 14, chance)
    merit = chance * count + jnp.arange(count)
    return lax.top_k(merit.astype(jnp.int32), top)[1].astype(jnp.int32)


def scatter_about(own_key, dims, deviation, bound, shards=(), kind=jnp.bfloat16):
    drawn = jax.random.normal(own_key, dims, jnp.float32) * deviation
    if len(shards) > 0:
        drawn = block_scale(own_key, dims, shards, -0.22, 0.18) * drawn
    return jnp.clip(drawn, min=-bound, max=bound).astype(kind)


def setup_inputs(seed: int = 0) -> dict:
    key_list = jax.random.split(jax.random.key(seed), 6)
    return {
        "tokens": scatter_about(key_list[0], (PATHS, PATH_TOKENS, D), 1.0, 6.0, ((0, 32), (1, 32))),
        "cotangent": scatter_about(key_list[1], (PATHS, PATH_TOKENS, R), 1.0, 6.0, ((0, 32), (1, 32))),
        "module_table": different_ones(key_list[2], PATHS, MODS, 1, 2048),
        "module_weights": scatter_about(key_list[3], (MODS, D, R), 1.0, 6.0, ((1, 32),)),
        "momentum": scatter_about(key_list[4], (MODS, D, R), 1.0, 6.0, ((1, 32),), jnp.float32),
    }


def path_delta(path_rows, path_cotangent, weights, step_size):
    latent = jnp.dot(path_rows, weights, preferred_element_type=jnp.float32)
    inverse_rms = lax.rsqrt(lax.optimization_barrier(jnp.mean(latent * latent, axis=-1, keepdims=True)) + 1e-06)
    normed = latent * inverse_rms
    upstream = path_cotangent.astype(jnp.float32)
    latent_cotangent = (inverse_rms * (upstream - normed * lax.optimization_barrier(jnp.mean(upstream * normed, axis=-1, keepdims=True)))).astype(jnp.bfloat16)
    gradient = lax.dot_general(path_rows, latent_cotangent, (((0,), (0,)), ((), ())), preferred_element_type=jnp.float32)
    return gradient * step_size

def reference(tokens, cotangent, module_table, module_weights, momentum):
    module_count = module_weights.shape[0]
    step_size = math.sqrt(D / PATH_TOKENS)
    choices_col = module_table[:, 0].astype(jnp.int32)
    module_ids = jnp.arange(module_count, dtype=jnp.int32)

    def accumulate(sums, items):
        path_rows, path_cotangent, module = items
        weights = lax.dynamic_index_in_dim(module_weights, module, 0, keepdims=False)
        delta = path_delta(path_rows, path_cotangent, weights, step_size)
        picked = (module_ids == module).astype(sums.dtype)
        return (sums + picked[:, None, None] * delta[None], None)
    start_sums = jnp.zeros(module_weights.shape, jnp.float32)
    sums, unused = lax.scan(accumulate, start_sums, (tokens, cotangent, choices_col))
    counts = lax.optimization_barrier(jnp.sum((choices_col[:, None] == module_ids[None, :]).astype(jnp.float32), axis=0))
    average = sums / counts[:, None, None]
    new_momentum = 0.9 * momentum + average
    new_weights = (module_weights.astype(jnp.float32) - 0.7 * (average + 0.9 * new_momentum)).astype(jnp.bfloat16)
    return (new_weights, new_momentum)
```

```python
import functools
import math

import jax
import jax.numpy as jnp
from jax import lax
from jax.experimental import pallas as pl
from jax.experimental.pallas import tpu as pltpu
from jax.sharding import PartitionSpec as P

MESH = pl.DeviceIdType.MESH
F32, BF16 = jnp.float32, jnp.bfloat16


def hops(nx):
    order = [0]
    for far in range(1, nx // 2 + 1):
        for signed in (far, -far):
            if signed % nx not in [d % nx for d in order]:
                order.append(signed)
    return order


def push(src, dst, sems, index, target):
    return pltpu.make_async_remote_copy(
        src_ref=src,
        dst_ref=dst,
        send_sem=sems.at[(0,) + index],
        recv_sem=sems.at[(1,) + index],
        device_id=target,
        device_id_type=MESH,
    )


def kernel(
    nx,
    paths,
    step_size,
    table,
    tok_hbm,
    ct_hbm,
    w_hbm,
    avg_ref,
    tok,
    ct,
    w,
    wall,
    latent,
    lct,
    acc,
    csend,
    crecv,
    zsend,
    zrecv,
    xsend,
    xrecv,
    slices,
    parts,
    gath,
    local_sem,
    ax,
    az,
    ac,
    bc,
    bz,
    bx,
    c1,
    c2,
):
    p = lax.axis_index("path")
    f = lax.axis_index("fsdp")
    c = lax.rem(f, 2)
    x = lax.rem(f // 2, nx)
    zl = f // (2 * nx)
    mods, rows, feats = w.shape
    toks = tok.shape[0]

    def at(z_of, x_of, c_of):
        return (z_of * nx + x_of) * 2 + c_of

    def along(d):
        return lax.rem(x + d + nx, nx)

    z_peer = (p, at(1 - zl, x, c))
    c_peer = (p, at(zl, x, 1 - c))

    loads = [
        pltpu.make_async_copy(src, dst, local_sem.at[i])
        for i, (src, dst) in enumerate(((w_hbm, w), (tok_hbm, tok), (ct_hbm, ct)))
    ]
    for load in loads:
        load.start()

    barrier = pltpu.get_barrier_semaphore()
    near = hops(nx)
    for d in near[1:]:
        pl.semaphore_signal(barrier, inc=1, device_id=(p, at(zl, along(d), c)), device_id_type=MESH)
    pl.semaphore_signal(barrier, inc=1, device_id=z_peer, device_id_type=MESH)
    pl.semaphore_signal(barrier, inc=1, device_id=c_peer, device_id_type=MESH)
    for r in range(1, paths):
        pl.semaphore_signal(barrier, inc=1, device_id=(lax.rem(p + r, paths), f), device_id_type=MESH)
    pl.semaphore_wait(barrier, nx - 1 + 2 + paths - 1)

    sent = []

    def start(copy):
        copy.start()
        sent.append(copy)
        return copy

    loads[0].wait()
    wall[f] = w[table[p]]
    for k, d in enumerate(near):
        if d:
            start(push(wall.at[f], wall.at[f], ax, (k,), (p, at(zl, along(d), c))))
    latent[...] = jnp.zeros_like(latent)
    loads[1].wait()

    def add_latent(chip):
        block = wall[pl.ds(chip * 2, 2)].reshape(2 * rows, feats)
        cols = pl.ds(pl.multiple_of(chip * 2 * rows, 2 * rows), 2 * rows)
        latent[...] += jnp.dot(tok[:, cols], block, preferred_element_type=F32)

    def gather_in(k):
        own = wall.at[at(zl, along(-near[k]), c)]
        if near[k]:
            push(own, own, ax, (k,), z_peer).wait_recv()
        start(push(own, own, az, (k,), z_peer))
        start(push(own, own, ac, (0, k), c_peer))

    def gather_pass(k):
        other = wall.at[at(1 - zl, along(-near[k]), c)]
        push(other, other, az, (k,), z_peer).wait_recv()
        start(push(other, other, ac, (1, k), c_peer))
        mate = wall.at[at(zl, along(-near[k]), 1 - c)]
        push(mate, mate, ac, (0, k), c_peer).wait_recv()
        add_latent(zl * nx + along(-near[k]))

    def gather_end(k):
        mate = wall.at[at(1 - zl, along(-near[k]), 1 - c)]
        push(mate, mate, ac, (1, k), c_peer).wait_recv()
        add_latent((1 - zl) * nx + along(-near[k]))

    for k in range(nx + 2):
        if k < nx:
            gather_in(k)
        if 0 <= k - 1 < nx:
            gather_pass(k - 1)
        if 0 <= k - 2 < nx:
            gather_end(k - 2)

    loads[2].wait()
    lat = latent[...]
    inverse_rms = lax.rsqrt(jnp.mean(lat * lat, axis=-1, keepdims=True) + 1e-06)
    normed = lat * inverse_rms
    upstream = ct[...].astype(F32)
    lc = inverse_rms * (upstream - normed * jnp.mean(upstream * normed, axis=-1, keepdims=True))
    lct[...] = lc.T.astype(BF16)

    far = near[::-1]

    def sum_cores(k):
        for cls in range(2):
            chip = (zl if cls == 0 else 1 - zl) * nx + along(far[k])
            cols = pl.ds(pl.multiple_of(chip * 2 * rows, 2 * rows), 2 * rows)
            grad = jnp.dot(lct[...], tok[:, cols], preferred_element_type=F32)
            first, second = grad[:, :rows], grad[:, rows:]
            acc[k, cls] = jnp.where(c == 0, first, second)
            csend[k, cls] = jnp.where(c == 0, second, first)
        start(push(csend.at[k], crecv.at[k], bc, (k,), c_peer))

    def sum_z(k):
        push(csend.at[k], crecv.at[k], bc, (k,), c_peer).wait_recv()
        zsend[k] = (acc[k, 1] + crecv[k, 1]).astype(BF16)
        start(push(zsend.at[k], zrecv.at[k], bz, (k,), z_peer))

    def sum_x(k):
        push(zsend.at[k], zrecv.at[k], bz, (k,), z_peer).wait_recv()
        total = acc[k, 0] + crecv[k, 0] + zrecv[k].astype(F32)
        if far[k]:
            xsend[k] = total.astype(BF16)
            start(push(xsend.at[k], xrecv.at[k], bx, (k,), (p, at(zl, along(far[k]), c))))
        else:
            acc[k, 0] = total

    for k in range(nx + 2):
        if k < nx:
            sum_cores(k)
        if 0 <= k - 1 < nx:
            sum_z(k - 1)
        if 0 <= k - 2 < nx:
            sum_x(k - 2)
    total = acc[nx - 1, 0]
    for k in range(nx - 1):
        push(xsend.at[k], xrecv.at[k], bx, (k,), z_peer).wait_recv()
        total += xrecv[k].astype(F32)

    piece = slices.shape[1]
    delta = total.T * step_size
    for q in range(paths):
        top = (q // 2) * piece
        slices[q] = delta[top : top + piece, (q % 2) * 128 : (q % 2) * 128 + 128]
    for r in range(1, paths):
        q = lax.rem(p + r, paths)
        start(push(slices.at[q], parts.at[p], c1, (r,), (q, f)))
    parts[p] = slices[p]
    for r in range(1, paths):
        source = lax.rem(p + paths - r, paths)
        push(slices.at[source], parts.at[source], c1, (r,), (source, f)).wait_recv()
    sums = []
    for m in range(mods):
        count = jnp.zeros((piece, 128), F32)
        summed = jnp.zeros((piece, 128), F32)
        for q in range(paths):
            picked = jnp.where(table[q] == m, 1.0, 0.0)
            count += picked
            summed += picked * parts[q]
        sums.append(summed / count)
    gath[p] = jnp.concatenate(sums, axis=0).astype(BF16)
    for r in range(1, paths):
        q = lax.rem(p + r, paths)
        start(push(gath.at[p], gath.at[p], c2, (r,), (q, f)))
    for r in range(1, paths):
        source = lax.rem(p + paths - r, paths)
        push(gath.at[source], gath.at[source], c2, (r,), (source, f)).wait_recv()
    lines = max(piece, 16)
    group = lines // piece
    for half in range(2):
        for top in range(0, rows, lines):
            blocks = [gath[(top // piece + i) * 2 + half].astype(F32) for i in range(group)]
            for m in range(mods):
                tile = [block[m * piece : (m + 1) * piece] for block in blocks]
                avg_ref[m, top : top + lines, half * 128 : half * 128 + 128] = jnp.concatenate(
                    tile, axis=0
                ).astype(BF16)
    for copy in sent:
        copy.wait_send()


def outer_update(weights, moment, average):
    new_moment = 0.9 * moment + average
    new_weights = (weights.astype(F32) - 0.7 * (average + 0.9 * new_moment)).astype(BF16)
    return (new_weights, new_moment)


def body(nx, paths, tokens, cotangent, module_table, module_weights, momentum):
    toks, width = tokens.shape[1:]
    mods, rows, feats = module_weights.shape
    step_size = math.sqrt(width / (toks * 4 * nx))
    piece = rows * feats // 128 // paths
    dma = pltpu.SemaphoreType.DMA
    average = pl.pallas_call(
        functools.partial(kernel, nx, paths, step_size),
        out_shape=jax.ShapeDtypeStruct((mods, rows, feats), BF16),
        in_specs=[pl.BlockSpec(memory_space=pltpu.SMEM)] + [pl.BlockSpec(memory_space=pl.ANY)] * 3,
        out_specs=pl.BlockSpec(memory_space=pltpu.VMEM),
        scratch_shapes=[
            pltpu.VMEM((toks, width), BF16),
            pltpu.VMEM((toks, feats), BF16),
            pltpu.VMEM((mods, rows, feats), BF16),
            pltpu.VMEM((4 * nx, rows, feats), BF16),
            pltpu.VMEM((toks, feats), F32),
            pltpu.VMEM((feats, toks), BF16),
            pltpu.VMEM((nx, 2, feats, rows), F32),
            pltpu.VMEM((nx, 2, feats, rows), F32),
            pltpu.VMEM((nx, 2, feats, rows), F32),
            pltpu.VMEM((nx, feats, rows), BF16),
            pltpu.VMEM((nx, feats, rows), BF16),
            pltpu.VMEM((nx, feats, rows), BF16),
            pltpu.VMEM((nx, feats, rows), BF16),
            pltpu.VMEM((paths, piece, 128), F32),
            pltpu.VMEM((paths, piece, 128), F32),
            pltpu.VMEM((paths, mods * piece, 128), BF16),
            dma((3,)),
            dma((2, nx)),
            dma((2, nx)),
            dma((2, 2, nx)),
            dma((2, nx)),
            dma((2, nx)),
            dma((2, nx)),
            dma((2, paths)),
            dma((2, paths)),
        ],
        compiler_params=pltpu.CompilerParams(
            collective_id=0, has_side_effects=True, vmem_limit_bytes=40 * 1024 * 1024
        ),
    )(module_table[:, 0], tokens[0], cotangent[0], module_weights)
    return outer_update(module_weights, momentum, average.astype(F32))


def solution(mesh):
    return jax.shard_map(
        functools.partial(body, mesh.shape["fsdp"] // 4, mesh.shape["path"]),
        mesh=mesh,
        in_specs=(
            P("path", "fsdp", None),
            P("path", "fsdp", None),
            P(),
            P(None, "fsdp", None),
            P(None, "fsdp", None),
        ),
        out_specs=(P(None, "fsdp", None), P(None, "fsdp", None)),
        check_vma=False,
    )
```

```python
import functools
import math

import jax
import jax.numpy as jnp
from jax import lax
from jax.experimental import pallas as pl
from jax.experimental.pallas import tpu as pltpu
from jax.sharding import PartitionSpec as P

MESH = pl.DeviceIdType.MESH
F32, BF16 = jnp.float32, jnp.bfloat16


GATHER = (0, 2, -2, 1, -1, 3, -3, 4)
SUM = (3, -3, 4, 1, -1, 2, -2, 0)
NEAR = (1, -1, 2, -2)


def push(src, dst, sems, index, target):
    return pltpu.make_async_remote_copy(
        src_ref=src,
        dst_ref=dst,
        send_sem=sems.at[(0,) + index],
        recv_sem=sems.at[(1,) + index],
        device_id=target,
        device_id_type=MESH,
    )


def kernel(
    nx,
    ny,
    nz,
    step_size,
    table,
    tok_hbm,
    ct_hbm,
    w_hbm,
    avg_ref,
    tok,
    ct,
    w,
    wall,
    latent,
    lct,
    acc,
    csend,
    crecv,
    zsend,
    zrecv,
    xsend,
    xrecv,
    slices,
    zparts,
    parts,
    zfirst,
    yfirst,
    local_sem,
    ax,
    az,
    ac,
    bc,
    bz,
    bx,
    c1z,
    c1y,
    c2z,
    c2y,
    c3z,
    c3y,
):
    p = lax.axis_index("path")
    f = lax.axis_index("fsdp")
    c = lax.rem(f, 2)
    x = lax.rem(f // 2, nx)
    zl = f // (2 * nx)
    y, z = p // nz, lax.rem(p, nz)
    paths = ny * nz
    mods, rows, feats = w.shape
    toks = tok.shape[0]

    def at(z_of, x_of, c_of):
        return (z_of * nx + x_of) * 2 + c_of

    def along(d):
        return lax.rem(x + d + nx, nx)

    z_peer = (p, at(1 - zl, x, c))
    c_peer = (p, at(zl, x, 1 - c))

    loads = [
        pltpu.make_async_copy(src, dst, local_sem.at[i])
        for i, (src, dst) in enumerate(((w_hbm, w), (tok_hbm, tok), (ct_hbm, ct)))
    ]
    for load in loads:
        load.start()

    barrier = pltpu.get_barrier_semaphore()
    for d in NEAR:
        pl.semaphore_signal(barrier, inc=1, device_id=(p, at(zl, along(d), c)), device_id_type=MESH)
    pl.semaphore_signal(barrier, inc=1, device_id=z_peer, device_id_type=MESH)
    pl.semaphore_signal(barrier, inc=1, device_id=c_peer, device_id_type=MESH)
    for r in range(1, nz):
        peer = (y * nz + lax.rem(z + r, nz), f)
        pl.semaphore_signal(barrier, inc=1, device_id=peer, device_id_type=MESH)
    for r in range(1, ny):
        peer = (lax.rem(y + r, ny) * nz + z, f)
        pl.semaphore_signal(barrier, inc=1, device_id=peer, device_id_type=MESH)
    pl.semaphore_wait(barrier, len(NEAR) + 2 + nz - 1 + ny - 1)

    sent = []

    def start(copy):
        copy.start()
        sent.append(copy)
        return copy

    loads[0].wait()
    wall[f] = w[table[p]]
    slot = {d: k for k, d in enumerate(GATHER)}
    side = 1 - 2 * c
    for d in (2, -2, 1, -1):
        start(push(wall.at[f], wall.at[f], ax, (slot[d],), (p, at(zl, along(d), c))))

    def half_latent(z_of):
        block = wall[pl.ds(z_of * 2 * nx, 2 * nx)].reshape(2 * nx * rows, feats)
        cols = pl.ds(pl.multiple_of(z_of * 2 * nx * rows, 2 * nx * rows), 2 * nx * rows)
        return jnp.dot(tok[:, cols], block, preferred_element_type=F32)

    def landed(block, d):
        push(block, block, ax, (slot[d],), z_peer).wait_recv()

    for k, d in enumerate(GATHER):
        own = wall.at[at(zl, along(-d), c)]
        if d == 2:
            other = wall.at[at(zl, along(2), c)]
            landed(own, 2)
            start(push(own, own, ax, (slot[3],), (p, at(zl, along(1), c))))
            landed(other, -2)
            start(push(other, other, ax, (slot[-3],), (p, at(zl, along(-1), c))))
            through = wall.at[at(zl, along(-2 * side), c)]
            start(push(through, through, ax, (slot[4],), (p, at(zl, along(2 * side), c))))
        elif d in (1, -1, 3, -3, 4):
            landed(own, d)
        start(push(own, own, az, (k,), z_peer))
        start(push(own, own, ac, (0, k), c_peer))
    for k, d in enumerate(GATHER):
        mate = wall.at[at(zl, along(-d), 1 - c)]
        push(mate, mate, ac, (0, k), c_peer).wait_recv()
    loads[1].wait()
    latent[...] = half_latent(zl)
    for k, d in enumerate(GATHER):
        other = wall.at[at(1 - zl, along(-d), c)]
        push(other, other, az, (k,), z_peer).wait_recv()
        start(push(other, other, ac, (1, k), c_peer))
    for k, d in enumerate(GATHER):
        mate = wall.at[at(1 - zl, along(-d), 1 - c)]
        push(mate, mate, ac, (1, k), c_peer).wait_recv()

    loads[2].wait()
    lat = latent[...] + half_latent(1 - zl)
    inverse_rms = lax.rsqrt(jnp.mean(lat * lat, axis=-1, keepdims=True) + 1e-06)
    normed = lat * inverse_rms
    upstream = ct[...].astype(F32)
    lc = inverse_rms * (upstream - normed * jnp.mean(upstream * normed, axis=-1, keepdims=True))
    lct[...] = lc.T.astype(BF16)

    def sum_cores(k):
        for cls in range(2):
            chip = (zl if cls == 0 else 1 - zl) * nx + along(SUM[k])
            cols = pl.ds(pl.multiple_of(chip * 2 * rows, 2 * rows), 2 * rows)
            grad = jnp.dot(lct[...], tok[:, cols], preferred_element_type=F32)
            first, second = grad[:, :rows], grad[:, rows:]
            acc[k, cls] = jnp.where(c == 0, first, second)
            csend[k, cls] = jnp.where(c == 0, second, first)
        start(push(csend.at[k], crecv.at[k], bc, (k,), c_peer))

    def sum_z(k):
        push(csend.at[k], crecv.at[k], bc, (k,), c_peer).wait_recv()
        zsend[k] = (acc[k, 1] + crecv[k, 1]).astype(BF16)
        start(push(zsend.at[k], zrecv.at[k], bz, (k,), z_peer))

    def sum_x(k):
        push(zsend.at[k], zrecv.at[k], bz, (k,), z_peer).wait_recv()
        total = acc[k, 0] + crecv[k, 0] + zrecv[k].astype(F32)
        d = SUM[k]
        if d == 2:
            arrived(0)
            arrived(2)
            total += xrecv[0].astype(F32) + jnp.where(c == 0, xrecv[2].astype(F32), 0.0)
        elif d == -2:
            arrived(1)
            total += xrecv[1].astype(F32) + jnp.where(c == 1, xrecv[2].astype(F32), 0.0)
        if d == 0:
            acc[k, 0] = total
            return
        step = {3: 1, -3: -1, 4: 2 * side}.get(d, d)
        xsend[k] = total.astype(BF16)
        start(push(xsend.at[k], xrecv.at[k], bx, (k,), (p, at(zl, along(step), c))))

    def arrived(k):
        push(xsend.at[k], xrecv.at[k], bx, (k,), z_peer).wait_recv()

    for k in range(nx + 4):
        if k < nx:
            sum_cores(k)
        if 0 <= k - 2 < nx:
            sum_z(k - 2)
        if 0 <= k - 4 < nx:
            sum_x(k - 4)
    total = acc[nx - 1, 0]
    for k in range(3, nx - 1):
        arrived(k)
        total += xrecv[k].astype(F32)

    piece = slices.shape[2]
    delta = total.T * step_size
    for q in range(paths):
        top = (q // 2) * piece
        slices[q % nz, q // nz] = delta[top : top + piece, (q % 2) * 128 : (q % 2) * 128 + 128]
    for r in range(1, nz):
        to = lax.rem(z + r, nz)
        start(push(slices.at[to], zparts.at[z], c1z, (r,), (y * nz + to, f)))
    zparts[z] = slices[z]
    for r in range(1, nz):
        push(zparts.at[z], zparts.at[lax.rem(z + nz - r, nz)], c1z, (r,), z_peer).wait_recv()
    for r in range(1, ny):
        to = lax.rem(y + r, ny)
        start(push(zparts.at[:, to], parts.at[y], c1y, (r,), (to * nz + z, f)))
    parts[y] = zparts[:, y]
    for r in range(1, ny):
        push(parts.at[y], parts.at[lax.rem(y + ny - r, ny)], c1y, (r,), z_peer).wait_recv()
    sums = []
    for m in range(mods):
        count = jnp.zeros((piece, 128), F32)
        summed = jnp.zeros((piece, 128), F32)
        for q in range(paths):
            picked = jnp.where(table[q] == m, 1.0, 0.0)
            count += picked
            summed += picked * parts[q // nz, q % nz]
        sums.append(summed / count)
    half = mods // 2
    zfirst[y, z] = jnp.concatenate(sums[:half], axis=0).astype(BF16)
    yfirst[z, y] = jnp.concatenate(sums[half:], axis=0).astype(BF16)

    def spread_z(buf, index, r, sems):
        return push(buf.at[index], buf.at[index], sems, (r,), (y * nz + lax.rem(z + r, nz), f))

    def spread_y(buf, index, r, sems):
        return push(buf.at[index], buf.at[index], sems, (r,), (lax.rem(y + r, ny) * nz + z, f))

    for r in range(1, nz):
        start(spread_z(zfirst, (y, z), r, c2z))
    for r in range(1, ny):
        start(spread_y(yfirst, (z, y), r, c2y))
    for r in range(1, nz):
        spread_z(zfirst, (y, lax.rem(z + nz - r, nz)), r, c2z).wait_recv()
    for r in range(1, ny):
        start(spread_y(zfirst, (y,), r, c3y))
    for r in range(1, ny):
        spread_y(yfirst, (z, lax.rem(y + ny - r, ny)), r, c2y).wait_recv()
    for r in range(1, nz):
        start(spread_z(yfirst, (z,), r, c3z))
    for r in range(1, ny):
        spread_y(zfirst, (lax.rem(y + ny - r, ny),), r, c3y).wait_recv()
    lines = max(piece, 16)
    group = lines // piece

    def unpack(first, block_of):
        for side in range(2):
            for top in range(0, rows, lines):
                blocks = [block_of((top // piece + i) * 2 + side) for i in range(group)]
                for m in range(half):
                    tile = [block[m * piece : (m + 1) * piece] for block in blocks]
                    avg_ref[first + m, top : top + lines, side * 128 : side * 128 + 128] = (
                        jnp.concatenate(tile, axis=0).astype(BF16)
                    )

    unpack(0, lambda q: zfirst[q // nz, q % nz].astype(F32))
    for r in range(1, nz):
        spread_z(yfirst, (lax.rem(z + nz - r, nz),), r, c3z).wait_recv()
    unpack(half, lambda q: yfirst[q % nz, q // nz].astype(F32))
    for copy in sent:
        copy.wait_send()


def outer_update(weights, moment, average):
    new_moment = 0.9 * moment + average
    new_weights = (weights.astype(F32) - 0.7 * (average + 0.9 * new_moment)).astype(BF16)
    return (new_weights, new_moment)


def body(nx, ny, nz, tokens, cotangent, module_table, module_weights, momentum):
    toks, width = tokens.shape[1:]
    mods, rows, feats = module_weights.shape
    step_size = math.sqrt(width / (toks * 4 * nx))
    piece = rows * feats // 128 // (ny * nz)
    dma = pltpu.SemaphoreType.DMA
    average = pl.pallas_call(
        functools.partial(kernel, nx, ny, nz, step_size),
        out_shape=jax.ShapeDtypeStruct((mods, rows, feats), BF16),
        in_specs=[pl.BlockSpec(memory_space=pltpu.SMEM)] + [pl.BlockSpec(memory_space=pltpu.HBM)] * 3,
        out_specs=pl.BlockSpec(memory_space=pltpu.VMEM),
        scratch_shapes=[
            pltpu.VMEM((toks, width), BF16),
            pltpu.VMEM((toks, feats), BF16),
            pltpu.VMEM((mods, rows, feats), BF16),
            pltpu.VMEM((4 * nx, rows, feats), BF16),
            pltpu.VMEM((toks, feats), F32),
            pltpu.VMEM((feats, toks), BF16),
            pltpu.VMEM((nx, 2, feats, rows), F32),
            pltpu.VMEM((nx, 2, feats, rows), F32),
            pltpu.VMEM((nx, 2, feats, rows), F32),
            pltpu.VMEM((nx, feats, rows), BF16),
            pltpu.VMEM((nx, feats, rows), BF16),
            pltpu.VMEM((nx, feats, rows), BF16),
            pltpu.VMEM((nx, feats, rows), BF16),
            pltpu.VMEM((nz, ny, piece, 128), F32),
            pltpu.VMEM((nz, ny, piece, 128), F32),
            pltpu.VMEM((ny, nz, piece, 128), F32),
            pltpu.VMEM((ny, nz, mods // 2 * piece, 128), BF16),
            pltpu.VMEM((nz, ny, mods // 2 * piece, 128), BF16),
            dma((3,)),
            dma((2, nx)),
            dma((2, nx)),
            dma((2, 2, nx)),
            dma((2, nx)),
            dma((2, nx)),
            dma((2, nx)),
            dma((2, nz)),
            dma((2, ny)),
            dma((2, nz)),
            dma((2, ny)),
            dma((2, nz)),
            dma((2, ny)),
        ],
        compiler_params=pltpu.CompilerParams(
            collective_id=0, has_side_effects=True, vmem_limit_bytes=62 * 1024 * 1024
        ),
    )(module_table[:, 0], tokens[0], cotangent[0], module_weights)
    return outer_update(module_weights, momentum, average.astype(F32))


def solution(mesh):
    paths = mesh.shape["path"]
    nz = 4 if paths >= 8 else max(paths // 2, 1)
    return jax.shard_map(
        functools.partial(body, mesh.shape["fsdp"] // 4, paths // nz, nz),
        mesh=mesh,
        in_specs=(
            P("path", "fsdp", None),
            P("path", "fsdp", None),
            P(),
            P(None, "fsdp", None),
            P(None, "fsdp", None),
        ),
        out_specs=(P(None, "fsdp", None), P(None, "fsdp", None)),
        check_vma=False,
    )
```

```python
import functools
import math

import jax
import jax.numpy as jnp
from jax import lax
from jax.experimental import pallas as pl
from jax.experimental.pallas import tpu as pltpu
from jax.sharding import PartitionSpec as P

MESH = pl.DeviceIdType.MESH
F32, BF16 = jnp.float32, jnp.bfloat16


GATHER = (0, 2, -2, 1, -1, 3, -3, 4)
SUM = (3, -3, 4, 1, -1, 2, -2, 0)
NEAR = (1, -1, 2, -2)


def push(src, dst, sems, index, target):
    return pltpu.make_async_remote_copy(
        src_ref=src,
        dst_ref=dst,
        send_sem=sems.at[(0,) + index],
        recv_sem=sems.at[(1,) + index],
        device_id=target,
        device_id_type=MESH,
    )


def kernel(
    nx,
    ny,
    nz,
    step_size,
    table_hbm,
    tok_hbm,
    ct_hbm,
    w_hbm,
    avg_ref,
    table,
    tok,
    ct,
    w,
    wall,
    latent,
    lct,
    acc,
    csend,
    crecv,
    zsend,
    zrecv,
    xsend,
    xrecv,
    slices,
    zparts,
    parts,
    zfirst,
    yfirst,
    ring,
    local_sem,
    ax,
    az,
    ac,
    bc,
    bz,
    bx,
    c1z,
    c1y,
    c2z,
    c2y,
    c3z,
    c3y,
):
    p = lax.axis_index("path")
    f = lax.axis_index("fsdp")
    c = lax.rem(f, 2)
    x = lax.rem(f // 2, nx)
    zl = f // (2 * nx)
    y, z = p // nz, lax.rem(p, nz)
    paths = ny * nz
    mods, rows, feats = w.shape
    toks = tok.shape[0]

    def at(z_of, x_of, c_of):
        return (z_of * nx + x_of) * 2 + c_of

    def along(d):
        return lax.rem(x + d + nx, nx)

    z_peer = (p, at(1 - zl, x, c))
    c_peer = (p, at(zl, x, 1 - c))

    loads = [
        pltpu.make_async_copy(src, dst, local_sem.at[i])
        for i, (src, dst) in enumerate(((w_hbm, w), (tok_hbm, tok), (ct_hbm, ct), (table_hbm, table)))
    ]
    for load in loads:
        load.start()

    barrier = pltpu.get_barrier_semaphore()
    for d in NEAR:
        pl.semaphore_signal(barrier, inc=1, device_id=(p, at(zl, along(d), c)), device_id_type=MESH)
    pl.semaphore_signal(barrier, inc=1, device_id=z_peer, device_id_type=MESH)
    pl.semaphore_signal(barrier, inc=1, device_id=c_peer, device_id_type=MESH)
    z_near = [(y * nz + lax.rem(z + r, nz), f) for r in (1, nz - 1)]
    y_near = [(lax.rem(y + r, ny) * nz + z, f) for r in (1, ny - 1)]
    for peer in z_near + y_near:
        pl.semaphore_signal(barrier, inc=1, device_id=peer, device_id_type=MESH)
    pl.semaphore_wait(barrier, len(NEAR) + 2 + 4)

    def tell(i, peers):
        for peer in peers:
            pl.semaphore_signal(ring.at[i], inc=1, device_id=peer, device_id_type=MESH)

    tell(3, z_near)
    tell(0, y_near)

    sent = []

    def start(copy):
        copy.start()
        sent.append(copy)
        return copy

    loads[3].wait()
    loads[0].wait()
    wall[f] = w[table[p]]
    slot = {d: k for k, d in enumerate(GATHER)}
    side = 1 - 2 * c
    for d in (2, -2, 1, -1):
        start(push(wall.at[f], wall.at[f], ax, (slot[d],), (p, at(zl, along(d), c))))

    def half_latent(z_of):
        block = wall[pl.ds(z_of * 2 * nx, 2 * nx)].reshape(2 * nx * rows, feats)
        cols = pl.ds(pl.multiple_of(z_of * 2 * nx * rows, 2 * nx * rows), 2 * nx * rows)
        return jnp.dot(tok[:, cols], block, preferred_element_type=F32)

    def landed(block, d):
        push(block, block, ax, (slot[d],), z_peer).wait_recv()

    for k, d in enumerate(GATHER):
        own = wall.at[at(zl, along(-d), c)]
        if d == 2:
            other = wall.at[at(zl, along(2), c)]
            landed(own, 2)
            start(push(own, own, ax, (slot[3],), (p, at(zl, along(1), c))))
            landed(other, -2)
            start(push(other, other, ax, (slot[-3],), (p, at(zl, along(-1), c))))
            through = wall.at[at(zl, along(-2 * side), c)]
            start(push(through, through, ax, (slot[4],), (p, at(zl, along(2 * side), c))))
        elif d in (1, -1, 3, -3, 4):
            landed(own, d)
        start(push(own, own, az, (k,), z_peer))
        start(push(own, own, ac, (0, k), c_peer))
    for k, d in enumerate(GATHER):
        mate = wall.at[at(zl, along(-d), 1 - c)]
        push(mate, mate, ac, (0, k), c_peer).wait_recv()
    pl.semaphore_wait(ring.at[0], 2)
    tell(1, y_near)
    loads[1].wait()
    latent[...] = half_latent(zl)
    for k, d in enumerate(GATHER):
        other = wall.at[at(1 - zl, along(-d), c)]
        push(other, other, az, (k,), z_peer).wait_recv()
        start(push(other, other, ac, (1, k), c_peer))
    for k, d in enumerate(GATHER):
        mate = wall.at[at(1 - zl, along(-d), 1 - c)]
        push(mate, mate, ac, (1, k), c_peer).wait_recv()

    pl.semaphore_wait(ring.at[1], 2)
    tell(2, y_near)

    loads[2].wait()
    lat = latent[...] + half_latent(1 - zl)
    inverse_rms = lax.rsqrt(jnp.mean(lat * lat, axis=-1, keepdims=True) + 1e-06)
    normed = lat * inverse_rms
    upstream = ct[...].astype(F32)
    lc = inverse_rms * (upstream - normed * jnp.mean(upstream * normed, axis=-1, keepdims=True))
    lct[...] = lc.T.astype(BF16)

    def sum_cores(k):
        for cls in range(2):
            chip = (zl if cls == 0 else 1 - zl) * nx + along(SUM[k])
            cols = pl.ds(pl.multiple_of(chip * 2 * rows, 2 * rows), 2 * rows)
            grad = jnp.dot(lct[...], tok[:, cols], preferred_element_type=F32)
            first, second = grad[:, :rows], grad[:, rows:]
            acc[k, cls] = jnp.where(c == 0, first, second)
            csend[k, cls] = jnp.where(c == 0, second, first)
        start(push(csend.at[k], crecv.at[k], bc, (k,), c_peer))

    def sum_z(k):
        push(csend.at[k], crecv.at[k], bc, (k,), c_peer).wait_recv()
        zsend[k] = (acc[k, 1] + crecv[k, 1]).astype(BF16)
        start(push(zsend.at[k], zrecv.at[k], bz, (k,), z_peer))

    def sum_x(k):
        push(zsend.at[k], zrecv.at[k], bz, (k,), z_peer).wait_recv()
        total = acc[k, 0] + crecv[k, 0] + zrecv[k].astype(F32)
        d = SUM[k]
        if d == 2:
            arrived(0)
            arrived(2)
            total += xrecv[0].astype(F32) + jnp.where(c == 0, xrecv[2].astype(F32), 0.0)
        elif d == -2:
            arrived(1)
            total += xrecv[1].astype(F32) + jnp.where(c == 1, xrecv[2].astype(F32), 0.0)
        if d == 0:
            acc[k, 0] = total
            return
        step = {3: 1, -3: -1, 4: 2 * side}.get(d, d)
        xsend[k] = total.astype(BF16)
        start(push(xsend.at[k], xrecv.at[k], bx, (k,), (p, at(zl, along(step), c))))

    def arrived(k):
        push(xsend.at[k], xrecv.at[k], bx, (k,), z_peer).wait_recv()

    for k in range(nx + 4):
        if k < nx:
            sum_cores(k)
        if 0 <= k - 2 < nx:
            sum_z(k - 2)
        if 0 <= k - 4 < nx:
            sum_x(k - 4)
    total = acc[nx - 1, 0]
    for k in range(3, nx - 1):
        arrived(k)
        total += xrecv[k].astype(F32)

    pl.semaphore_wait(ring.at[2], 2)
    pl.semaphore_wait(ring.at[3], 2)

    piece = slices.shape[2]
    delta = total.T * step_size
    for q in range(paths):
        top = (q // 2) * piece
        slices[q % nz, q // nz] = delta[top : top + piece, (q % 2) * 128 : (q % 2) * 128 + 128]
    z_far = sorted(range(1, nz), key=lambda r: -min(r, nz - r))
    y_far = sorted(range(1, ny), key=lambda r: -min(r, ny - r))
    for r in z_far:
        to = lax.rem(z + r, nz)
        start(push(slices.at[to], zparts.at[z], c1z, (r,), (y * nz + to, f)))
    zparts[z] = slices[z]
    for r in range(1, nz):
        push(zparts.at[z], zparts.at[lax.rem(z + nz - r, nz)], c1z, (r,), z_peer).wait_recv()
    for r in y_far:
        to = lax.rem(y + r, ny)
        start(push(zparts.at[:, to], parts.at[y], c1y, (r,), (to * nz + z, f)))
    parts[y] = zparts[:, y]
    for r in range(1, ny):
        push(parts.at[y], parts.at[lax.rem(y + ny - r, ny)], c1y, (r,), z_peer).wait_recv()
    sums = []
    for m in range(mods):
        count = jnp.zeros((piece, 128), F32)
        summed = jnp.zeros((piece, 128), F32)
        for q in range(paths):
            picked = jnp.where(table[q] == m, 1.0, 0.0)
            count += picked
            summed += picked * parts[q // nz, q % nz]
        sums.append(summed / count)
    half = mods // 2
    zfirst[y, z] = jnp.concatenate(sums[:half], axis=0).astype(BF16)
    yfirst[z, y] = jnp.concatenate(sums[half:], axis=0).astype(BF16)

    def spread_z(buf, index, r, sems):
        return push(buf.at[index], buf.at[index], sems, (r,), (y * nz + lax.rem(z + r, nz), f))

    def spread_y(buf, index, r, sems):
        return push(buf.at[index], buf.at[index], sems, (r,), (lax.rem(y + r, ny) * nz + z, f))

    for r in z_far:
        start(spread_z(zfirst, (y, z), r, c2z))
    for r in y_far:
        start(spread_y(yfirst, (z, y), r, c2y))
    for r in range(1, nz):
        spread_z(zfirst, (y, lax.rem(z + nz - r, nz)), r, c2z).wait_recv()
    for r in y_far:
        start(spread_y(zfirst, (y,), r, c3y))
    for r in range(1, ny):
        spread_y(yfirst, (z, lax.rem(y + ny - r, ny)), r, c2y).wait_recv()
    for r in z_far:
        start(spread_z(yfirst, (z,), r, c3z))
    for r in range(1, ny):
        spread_y(zfirst, (lax.rem(y + ny - r, ny),), r, c3y).wait_recv()
    lines = max(piece, 16)
    group = lines // piece

    def unpack(first, block_of):
        for side in range(2):
            for top in range(0, rows, lines):
                blocks = [block_of((top // piece + i) * 2 + side) for i in range(group)]
                for m in range(half):
                    tile = [block[m * piece : (m + 1) * piece] for block in blocks]
                    avg_ref[first + m, top : top + lines, side * 128 : side * 128 + 128] = (
                        jnp.concatenate(tile, axis=0).astype(BF16)
                    )

    unpack(0, lambda q: zfirst[q // nz, q % nz].astype(F32))
    for r in range(1, nz):
        spread_z(yfirst, (lax.rem(z + nz - r, nz),), r, c3z).wait_recv()
    unpack(half, lambda q: yfirst[q % nz, q // nz].astype(F32))
    for copy in sent:
        copy.wait_send()


def outer_update(weights, moment, average):
    new_moment = 0.9 * moment + average
    new_weights = (weights.astype(F32) - 0.7 * (average + 0.9 * new_moment)).astype(BF16)
    return (new_weights, new_moment)


def body(nx, ny, nz, tokens, cotangent, module_table, module_weights, momentum):
    toks, width = tokens.shape[1:]
    mods, rows, feats = module_weights.shape
    step_size = math.sqrt(width / (toks * 4 * nx))
    piece = rows * feats // 128 // (ny * nz)
    dma = pltpu.SemaphoreType.DMA
    average = pl.pallas_call(
        functools.partial(kernel, nx, ny, nz, step_size),
        out_shape=jax.ShapeDtypeStruct((mods, rows, feats), BF16),
        in_specs=[pl.BlockSpec(memory_space=pltpu.HBM)] * 4,
        out_specs=pl.BlockSpec(memory_space=pltpu.VMEM),
        scratch_shapes=[
            pltpu.SMEM((ny * nz,), jnp.int32),
            pltpu.VMEM((toks, width), BF16),
            pltpu.VMEM((toks, feats), BF16),
            pltpu.VMEM((mods, rows, feats), BF16),
            pltpu.VMEM((4 * nx, rows, feats), BF16),
            pltpu.VMEM((toks, feats), F32),
            pltpu.VMEM((feats, toks), BF16),
            pltpu.VMEM((nx, 2, feats, rows), F32),
            pltpu.VMEM((nx, 2, feats, rows), F32),
            pltpu.VMEM((nx, 2, feats, rows), F32),
            pltpu.VMEM((nx, feats, rows), BF16),
            pltpu.VMEM((nx, feats, rows), BF16),
            pltpu.VMEM((nx, feats, rows), BF16),
            pltpu.VMEM((nx, feats, rows), BF16),
            pltpu.VMEM((nz, ny, piece, 128), F32),
            pltpu.VMEM((nz, ny, piece, 128), F32),
            pltpu.VMEM((ny, nz, piece, 128), F32),
            pltpu.VMEM((ny, nz, mods // 2 * piece, 128), BF16),
            pltpu.VMEM((nz, ny, mods // 2 * piece, 128), BF16),
            pltpu.SemaphoreType.REGULAR((4,)),
            dma((4,)),
            dma((2, nx)),
            dma((2, nx)),
            dma((2, 2, nx)),
            dma((2, nx)),
            dma((2, nx)),
            dma((2, nx)),
            dma((2, nz)),
            dma((2, ny)),
            dma((2, nz)),
            dma((2, ny)),
            dma((2, nz)),
            dma((2, ny)),
        ],
        compiler_params=pltpu.CompilerParams(
            collective_id=0, has_side_effects=True, vmem_limit_bytes=50 * 1024 * 1024
        ),
    )(*[pltpu.with_memory_space_constraint(a, pltpu.HBM) for a in (module_table[:, 0], tokens[0], cotangent[0], module_weights)])
    return outer_update(module_weights, momentum, average.astype(F32))


def solution(mesh):
    paths = mesh.shape["path"]
    nz = 4 if paths >= 8 else max(paths // 2, 1)
    return jax.shard_map(
        functools.partial(body, mesh.shape["fsdp"] // 4, paths // nz, nz),
        mesh=mesh,
        in_specs=(
            P("path", "fsdp", None),
            P("path", "fsdp", None),
            P(),
            P(None, "fsdp", None),
            P(None, "fsdp", None),
        ),
        out_specs=(P(None, "fsdp", None), P(None, "fsdp", None)),
        check_vma=False,
    )
```

```python
import functools
import math

import jax
import jax.numpy as jnp
from jax import lax
from jax.experimental import pallas as pl
from jax.experimental.pallas import tpu as pltpu
from jax.sharding import PartitionSpec as P

MESH = pl.DeviceIdType.MESH
F32, BF16 = jnp.float32, jnp.bfloat16


GATHER = (0, 2, -2, 1, -1, 3, -3, 4)
SUM = (3, -3, 4, 1, -1, 2, -2, 0)
NEAR = (1, -1, 2, -2)


def push(src, dst, sems, index, target):
    return pltpu.make_async_remote_copy(
        src_ref=src,
        dst_ref=dst,
        send_sem=sems.at[(0,) + index],
        recv_sem=sems.at[(1,) + index],
        device_id=target,
        device_id_type=MESH,
    )


def kernel(
    nx,
    ny,
    nz,
    step_size,
    table_hbm,
    tok_hbm,
    ct_hbm,
    w_hbm,
    avg_ref,
    table,
    tok,
    ct,
    w,
    wall,
    latent,
    lct,
    acc,
    csend,
    crecv,
    zsend,
    zrecv,
    xsend,
    xrecv,
    slices,
    zparts,
    parts,
    picks,
    counts,
    zfirst,
    yfirst,
    ring,
    local_sem,
    ax,
    az,
    ac,
    bc,
    bz,
    bx,
    c1z,
    c1y,
    c2z,
    c2y,
    c3z,
    c3y,
):
    p = lax.axis_index("path")
    f = lax.axis_index("fsdp")
    c = lax.rem(f, 2)
    x = lax.rem(f // 2, nx)
    zl = f // (2 * nx)
    y, z = p // nz, lax.rem(p, nz)
    paths = ny * nz
    mods, rows, feats = w.shape
    toks = tok.shape[0]

    def at(z_of, x_of, c_of):
        return (z_of * nx + x_of) * 2 + c_of

    def along(d):
        return lax.rem(x + d + nx, nx)

    z_peer = (p, at(1 - zl, x, c))
    c_peer = (p, at(zl, x, 1 - c))

    loads = [
        pltpu.make_async_copy(src, dst, local_sem.at[i])
        for i, (src, dst) in enumerate(((w_hbm, w), (tok_hbm, tok), (ct_hbm, ct), (table_hbm, table)))
    ]
    for load in loads:
        load.start()

    barrier = pltpu.get_barrier_semaphore()
    for d in NEAR:
        pl.semaphore_signal(barrier, inc=1, device_id=(p, at(zl, along(d), c)), device_id_type=MESH)
    pl.semaphore_signal(barrier, inc=1, device_id=z_peer, device_id_type=MESH)
    pl.semaphore_signal(barrier, inc=1, device_id=c_peer, device_id_type=MESH)
    z_near = [(y * nz + lax.rem(z + r, nz), f) for r in (1, nz - 1)]
    y_near = [(lax.rem(y + r, ny) * nz + z, f) for r in (1, ny - 1)]
    for peer in z_near + y_near:
        pl.semaphore_signal(barrier, inc=1, device_id=peer, device_id_type=MESH)
    pl.semaphore_wait(barrier, len(NEAR) + 2 + 4)

    def tell(i, peers):
        for peer in peers:
            pl.semaphore_signal(ring.at[i], inc=1, device_id=peer, device_id_type=MESH)

    tell(3, z_near)
    tell(0, y_near)

    sent = []

    def start(copy):
        copy.start()
        sent.append(copy)
        return copy

    loads[3].wait()
    loads[0].wait()
    wall[f] = w[table[p]]
    slot = {d: k for k, d in enumerate(GATHER)}
    side = 1 - 2 * c
    for d in (2, -2, 1, -1):
        start(push(wall.at[f], wall.at[f], ax, (slot[d],), (p, at(zl, along(d), c))))

    def half_latent(z_of):
        block = wall[pl.ds(z_of * 2 * nx, 2 * nx)].reshape(2 * nx * rows, feats)
        cols = pl.ds(pl.multiple_of(z_of * 2 * nx * rows, 2 * nx * rows), 2 * nx * rows)
        return jnp.dot(tok[:, cols], block, preferred_element_type=F32)

    def landed(block, d):
        push(block, block, ax, (slot[d],), z_peer).wait_recv()

    for k, d in enumerate(GATHER):
        own = wall.at[at(zl, along(-d), c)]
        if d == 2:
            other = wall.at[at(zl, along(2), c)]
            landed(own, 2)
            start(push(own, own, ax, (slot[3],), (p, at(zl, along(1), c))))
            landed(other, -2)
            start(push(other, other, ax, (slot[-3],), (p, at(zl, along(-1), c))))
            through = wall.at[at(zl, along(-2 * side), c)]
            start(push(through, through, ax, (slot[4],), (p, at(zl, along(2 * side), c))))
        elif d in (1, -1, 3, -3, 4):
            landed(own, d)
        start(push(own, own, az, (k,), z_peer))
        start(push(own, own, ac, (0, k), c_peer))
    pl.semaphore_wait(ring.at[0], 2)
    tell(1, y_near)
    for k, d in enumerate(GATHER):
        other = wall.at[at(1 - zl, along(-d), c)]
        push(other, other, az, (k,), z_peer).wait_recv()
        start(push(other, other, ac, (1, k), c_peer))
    for k, d in enumerate(GATHER):
        mate = wall.at[at(zl, along(-d), 1 - c)]
        push(mate, mate, ac, (0, k), c_peer).wait_recv()
    loads[1].wait()
    latent[...] = half_latent(zl)
    for k, d in enumerate(GATHER):
        mate = wall.at[at(1 - zl, along(-d), 1 - c)]
        push(mate, mate, ac, (1, k), c_peer).wait_recv()

    pl.semaphore_wait(ring.at[1], 2)
    tell(2, y_near)

    loads[2].wait()
    lat = latent[...] + half_latent(1 - zl)
    inverse_rms = lax.rsqrt(jnp.mean(lat * lat, axis=-1, keepdims=True) + 1e-06)
    normed = lat * inverse_rms
    upstream = ct[...].astype(F32)
    lc = inverse_rms * (upstream - normed * jnp.mean(upstream * normed, axis=-1, keepdims=True))
    lct[...] = lc.T.astype(BF16)

    def sum_cores(k):
        for cls in range(2):
            chip = (zl if cls == 0 else 1 - zl) * nx + along(SUM[k])
            cols = pl.ds(pl.multiple_of(chip * 2 * rows, 2 * rows), 2 * rows)
            grad = jnp.dot(lct[...], tok[:, cols], preferred_element_type=F32)
            first, second = grad[:, :rows], grad[:, rows:]
            acc[k, cls] = jnp.where(c == 0, first, second)
            csend[k, cls] = jnp.where(c == 0, second, first)
        start(push(csend.at[k], crecv.at[k], bc, (k,), c_peer))

    def sum_z(k):
        push(csend.at[k], crecv.at[k], bc, (k,), c_peer).wait_recv()
        zsend[k] = (acc[k, 1] + crecv[k, 1]).astype(BF16)
        start(push(zsend.at[k], zrecv.at[k], bz, (k,), z_peer))

    def sum_x(k):
        push(zsend.at[k], zrecv.at[k], bz, (k,), z_peer).wait_recv()
        total = acc[k, 0] + crecv[k, 0] + zrecv[k].astype(F32)
        d = SUM[k]
        if d == 2:
            arrived(0)
            arrived(2)
            total += xrecv[0].astype(F32) + jnp.where(c == 0, xrecv[2].astype(F32), 0.0)
        elif d == -2:
            arrived(1)
            total += xrecv[1].astype(F32) + jnp.where(c == 1, xrecv[2].astype(F32), 0.0)
        if d == 0:
            acc[k, 0] = total
            return
        step = {3: 1, -3: -1, 4: 2 * side}.get(d, d)
        xsend[k] = total.astype(BF16)
        start(push(xsend.at[k], xrecv.at[k], bx, (k,), (p, at(zl, along(step), c))))

    def arrived(k):
        push(xsend.at[k], xrecv.at[k], bx, (k,), z_peer).wait_recv()

    for k in range(nx + 4):
        if k < nx:
            sum_cores(k)
        if 0 <= k - 2 < nx:
            sum_z(k - 2)
        if 0 <= k - 4 < nx:
            sum_x(k - 4)
    total = acc[nx - 1, 0]
    for k in range(3, nx - 1):
        arrived(k)
        total += xrecv[k].astype(F32)

    pl.semaphore_wait(ring.at[2], 2)
    pl.semaphore_wait(ring.at[3], 2)

    piece = slices.shape[2]
    delta = total.T * step_size
    for q in range(paths):
        top = (q // 2) * piece
        slices[q % nz, q // nz] = delta[top : top + piece, (q % 2) * 128 : (q % 2) * 128 + 128]
    def settle(count):
        for _ in range(count):
            sent.pop(0).wait_send()

    before = len(sent)
    z_far = sorted(range(1, nz), key=lambda r: -min(r, nz - r))
    y_far = sorted(range(1, ny), key=lambda r: -min(r, ny - r))
    for r in z_far:
        to = lax.rem(z + r, nz)
        start(push(slices.at[to], zparts.at[z], c1z, (r,), (y * nz + to, f)))
    zparts[z] = slices[z]
    settle(before)
    for m in range(mods):
        count = jnp.zeros((piece, 128), F32)
        for q in range(paths):
            picks[m, q] = jnp.full((piece, 128), jnp.where(table[q] == m, 1.0, 0.0))
            count += picks[m, q]
        counts[m] = count
    for r in range(1, nz):
        push(zparts.at[z], zparts.at[lax.rem(z + nz - r, nz)], c1z, (r,), z_peer).wait_recv()
    for r in y_far:
        to = lax.rem(y + r, ny)
        start(push(zparts.at[:, to], parts.at[y], c1y, (r,), (to * nz + z, f)))
    parts[y] = zparts[:, y]
    for r in range(1, ny):
        push(parts.at[y], parts.at[lax.rem(y + ny - r, ny)], c1y, (r,), z_peer).wait_recv()
    sums = []
    for m in range(mods):
        summed = jnp.zeros((piece, 128), F32)
        for q in range(paths):
            summed += picks[m, q] * parts[q // nz, q % nz]
        sums.append(summed / counts[m])
    half = mods // 2
    before = len(sent)
    zfirst[y, z] = jnp.concatenate(sums[:half], axis=0).astype(BF16)
    yfirst[z, y] = jnp.concatenate(sums[half:], axis=0).astype(BF16)

    def spread_z(buf, index, r, sems):
        return push(buf.at[index], buf.at[index], sems, (r,), (y * nz + lax.rem(z + r, nz), f))

    def spread_y(buf, index, r, sems):
        return push(buf.at[index], buf.at[index], sems, (r,), (lax.rem(y + r, ny) * nz + z, f))

    for r in z_far:
        start(spread_z(zfirst, (y, z), r, c2z))
    for r in y_far:
        start(spread_y(yfirst, (z, y), r, c2y))
    for r in range(1, nz):
        spread_z(zfirst, (y, lax.rem(z + nz - r, nz)), r, c2z).wait_recv()
    for r in y_far:
        start(spread_y(zfirst, (y,), r, c3y))
    for r in range(1, ny):
        spread_y(yfirst, (z, lax.rem(y + ny - r, ny)), r, c2y).wait_recv()
    for r in z_far:
        start(spread_z(yfirst, (z,), r, c3z))
    settle(before + ny + nz - 2)
    for r in range(1, ny):
        spread_y(zfirst, (lax.rem(y + ny - r, ny),), r, c3y).wait_recv()
    lines = max(piece, 16)
    group = lines // piece

    def unpack(first, block_of):
        for side in range(2):
            for top in range(0, rows, lines):
                blocks = [block_of((top // piece + i) * 2 + side) for i in range(group)]
                for m in range(half):
                    tile = [block[m * piece : (m + 1) * piece] for block in blocks]
                    avg_ref[first + m, top : top + lines, side * 128 : side * 128 + 128] = (
                        jnp.concatenate(tile, axis=0).astype(BF16)
                    )

    unpack(0, lambda q: zfirst[q // nz, q % nz].astype(F32))
    for r in range(1, nz):
        spread_z(yfirst, (lax.rem(z + nz - r, nz),), r, c3z).wait_recv()
    unpack(half, lambda q: yfirst[q % nz, q // nz].astype(F32))
    for copy in sent:
        copy.wait_send()


def outer_update(weights, moment, average):
    new_moment = 0.9 * moment + average
    new_weights = (weights.astype(F32) - 0.7 * (average + 0.9 * new_moment)).astype(BF16)
    return (new_weights, new_moment)


def body(nx, ny, nz, tokens, cotangent, module_table, module_weights, momentum):
    toks, width = tokens.shape[1:]
    mods, rows, feats = module_weights.shape
    step_size = math.sqrt(width / (toks * 4 * nx))
    piece = rows * feats // 128 // (ny * nz)
    dma = pltpu.SemaphoreType.DMA
    average = pl.pallas_call(
        functools.partial(kernel, nx, ny, nz, step_size),
        out_shape=jax.ShapeDtypeStruct((mods, rows, feats), BF16),
        in_specs=[pl.BlockSpec(memory_space=pltpu.HBM)] * 4,
        out_specs=pl.BlockSpec(memory_space=pltpu.VMEM),
        scratch_shapes=[
            pltpu.SMEM((ny * nz,), jnp.int32),
            pltpu.VMEM((toks, width), BF16),
            pltpu.VMEM((toks, feats), BF16),
            pltpu.VMEM((mods, rows, feats), BF16),
            pltpu.VMEM((4 * nx, rows, feats), BF16),
            pltpu.VMEM((toks, feats), F32),
            pltpu.VMEM((feats, toks), BF16),
            pltpu.VMEM((nx, 2, feats, rows), F32),
            pltpu.VMEM((nx, 2, feats, rows), F32),
            pltpu.VMEM((nx, 2, feats, rows), F32),
            pltpu.VMEM((nx, feats, rows), BF16),
            pltpu.VMEM((nx, feats, rows), BF16),
            pltpu.VMEM((nx, feats, rows), BF16),
            pltpu.VMEM((nx, feats, rows), BF16),
            pltpu.VMEM((nz, ny, piece, 128), F32),
            pltpu.VMEM((nz, ny, piece, 128), F32),
            pltpu.VMEM((ny, nz, piece, 128), F32),
            pltpu.VMEM((mods, ny * nz, piece, 128), F32),
            pltpu.VMEM((mods, piece, 128), F32),
            pltpu.VMEM((ny, nz, mods // 2 * piece, 128), BF16),
            pltpu.VMEM((nz, ny, mods // 2 * piece, 128), BF16),
            pltpu.SemaphoreType.REGULAR((4,)),
            dma((4,)),
            dma((2, nx)),
            dma((2, nx)),
            dma((2, 2, nx)),
            dma((2, nx)),
            dma((2, nx)),
            dma((2, nx)),
            dma((2, nz)),
            dma((2, ny)),
            dma((2, nz)),
            dma((2, ny)),
            dma((2, nz)),
            dma((2, ny)),
        ],
        compiler_params=pltpu.CompilerParams(
            collective_id=0, has_side_effects=True, vmem_limit_bytes=50 * 1024 * 1024
        ),
    )(*[pltpu.with_memory_space_constraint(a, pltpu.HBM) for a in (module_table[:, 0], tokens[0], cotangent[0], module_weights)])
    return outer_update(module_weights, momentum, average.astype(F32))


def solution(mesh):
    paths = mesh.shape["path"]
    nz = 4 if paths >= 8 else max(paths // 2, 1)
    return jax.shard_map(
        functools.partial(body, mesh.shape["fsdp"] // 4, paths // nz, nz),
        mesh=mesh,
        in_specs=(
            P("path", "fsdp", None),
            P("path", "fsdp", None),
            P(),
            P(None, "fsdp", None),
            P(None, "fsdp", None),
        ),
        out_specs=(P(None, "fsdp", None), P(None, "fsdp", None)),
        check_vma=False,
    )
```
